32 devices in a mesh: fsdp: 2 (over y), ctx: 4 (over z), tp: 4 (over x, core).
Axes of the slice: x: 2, y: 2, z: 4, core: 2. Of those that a mesh axis runs over, the one named last changes fastest.
Arguments:
- latent_in: bfloat16 [4, 1024, 768], P('fsdp', 'ctx'), may hold values from -6 to 6
- condition: bfloat16 [4, 768], P('fsdp'), may hold values from -6 to 6
- ada_weight: bfloat16 [768, 6, 768], P('fsdp', None, 'tp'), may hold values from -0.21875 to 0.21875
- ada_bias: float32 [6, 768], P(None, 'tp'), may hold values from -3 to 3
- qkv_weight: bfloat16 [768, 3, 768], P('fsdp', None, 'tp'), may hold values from -0.21875 to 0.21875
- qv_bias: float32 [2, 768], P(None, 'tp'), may hold values from -3 to 3
- out_weight: bfloat16 [768, 768], P('fsdp', 'tp'), may hold values from -2.5 to 2.5
- out_bias: float32 [768], replicated, may hold values from -3 to 3
- fc1_weight: bfloat16 [768, 3072], P('fsdp', 'tp'), may hold values from -0.21875 to 0.21875
- fc1_bias: float32 [3072], P('tp'), may hold values from -3 to 3
- fc2_weight: bfloat16 [768, 3072], P('fsdp', 'tp'), may hold values from -0.109375 to 0.109375
- fc2_bias: float32 [768], replicated, may hold values from -3 to 3
- out_grad: float32 [4, 1024, 768], P('fsdp', 'ctx'), may hold values from -6 to 6
Outputs:
- block_out: float32 [4, 1024, 768], P('fsdp', 'ctx')
- latent_grad: float32 [4, 1024, 768], P('fsdp', 'ctx')
- condition_grad: float32 [4, 768], P('fsdp')
- ada_weight_grad: float32 [768, 6, 768], P('fsdp', None, 'tp')
- ada_bias_grad: float32 [6, 768], P(None, 'tp')
- qkv_weight_grad: float32 [768, 3, 768], P('fsdp', None, 'tp')
- qv_bias_grad: float32 [2, 768], P(None, 'tp')
- out_weight_grad: float32 [768, 768], P('fsdp', 'tp')
- out_bias_grad: float32 [768], replicated
- fc1_weight_grad: float32 [768, 3072], P('fsdp', 'tp')
- fc1_bias_grad: float32 [3072], P('tp')
- fc2_weight_grad: float32 [768, 3072], P('fsdp', 'tp')
- fc2_bias_grad: float32 [768], replicated
The draws below stay inside these ranges and needn't reach their ends.
All inputs are finite; a program needn't handle non-finite values.
Results may differ from the reference program's by a relative error of at most 0.009.
The reference program's roundings to bfloat16 on the way count: a program that leaves them out, or rounds other values in their place, can miss the bound.
Values may be sent and summed in bfloat16 or wider, within the bound.
A program may use at most 128 MiB of HBM per device.

```python
import jax
import jax.numpy as jnp
from jax import lax

D = 768
HEADS = 12
HEAD_DIM = 64
FF = 3072
SEQ = 1024
LATENTS = 4


def block_scale(stream_key, shape, split, smallest, top_value):
    gain = 1.0
    for axis_at, blocks in split:
        heights = jax.random.uniform(jax.random.fold_in(jax.random.fold_in(stream_key, 6), axis_at), (blocks,), jnp.float32, smallest / len(split), top_value / len(split))
        gain = gain * jnp.repeat(jnp.exp(heights), shape[axis_at] // blocks).reshape((-1,) + (1,) * (len(shape) - 1 - axis_at))
    return gain


def centred(rng, shape, scale, limit, split=(), dtype=jnp.bfloat16):
    drawn = jax.random.normal(rng, shape, jnp.float32) * scale
    if len(split) > 0:
        drawn = block_scale(rng, shape, split, -0.22, 0.18) * drawn
    return jnp.clip(drawn, min=-limit, max=limit).astype(dtype)


def setup_inputs(seed: int = 0) -> dict:
    seeds = jax.random.split(jax.random.key(seed), 14)
    latent_in = centred(seeds[0], (LATENTS, SEQ, D), 1.0, 6.0, ((0, 2), (1, 4)))
    condition = centred(seeds[1], (LATENTS, D), 1.0, 6.0, ((0, 2),))
    ada_weight = centred(seeds[2], (D, 6, D), D ** -0.5, 0.21875, ((0, 2), (2, 4)))
    ada_bias = centred(seeds[3], (6, D), 0.5, 3.0, ((1, 4),), jnp.float32)
    qkv_weight = centred(seeds[4], (D, 3, D), D ** -0.5, 0.21875, ((0, 2), (2, 4)))
    qv_bias = centred(seeds[5], (2, D), 0.5, 3.0, ((1, 4),), jnp.float32)
    out_weight = centred(seeds[6], (D, D), (max(D // 128, 2)) ** -0.5, 2.5, ((0, 2), (1, 4)))
    out_bias = centred(seeds[7], (D,), 0.5, 3.0, (), jnp.float32)
    fc1_weight = centred(seeds[8], (D, FF), D ** -0.5, 0.21875, ((0, 2), (1, 4)))
    fc1_bias = centred(seeds[9], (FF,), 0.5, 3.0, ((0, 4),), jnp.float32)
    fc2_weight = centred(seeds[10], (D, FF), FF ** -0.5, 0.109375, ((0, 2), (1, 4)))
    fc2_bias = centred(seeds[11], (D,), 0.5, 3.0, (), jnp.float32)
    out_grad = centred(seeds[12], (LATENTS, SEQ, D), 1.0, 6.0, ((0, 2), (1, 4)), jnp.float32)
    return dict(latent_in=latent_in, condition=condition, ada_weight=ada_weight, ada_bias=ada_bias, qkv_weight=qkv_weight, qv_bias=qv_bias, out_weight=out_weight, out_bias=out_bias, fc1_weight=fc1_weight, fc1_bias=fc1_bias, fc2_weight=fc2_weight, fc2_bias=fc2_bias, out_grad=out_grad)


EPS = 1e-06

def dot32(left, right):
    return jnp.dot(left, right, preferred_element_type=jnp.float32)

def as_float(values):
    return lax.optimization_barrier(values).astype(jnp.float32)

def norm_rows(values):
    centre = lax.optimization_barrier(jnp.mean(values, axis=-1, keepdims=True))
    shifted = values - centre
    spread = lax.optimization_barrier(jnp.mean(shifted * shifted, axis=-1, keepdims=True))
    inverse = lax.rsqrt(spread + EPS)
    return (shifted * inverse, inverse)

def norm_back(grad_norm, normed, inverse):
    first = lax.optimization_barrier(jnp.mean(grad_norm, axis=-1, keepdims=True))
    second = lax.optimization_barrier(jnp.mean(grad_norm * normed, axis=-1, keepdims=True))
    return inverse * (grad_norm - first - normed * second)

def gelu_fn(values):
    return jax.nn.gelu(values, approximate=True)

def reference(latent_in, condition, ada_weight, ada_bias, qkv_weight, qv_bias, out_weight, out_bias, fc1_weight, fc1_bias, fc2_weight, fc2_bias, out_grad):
    att_scale = HEAD_DIM ** (-0.5)
    ada_flat = ada_weight.reshape(D, 6 * D)
    qkv_flat = qkv_weight.reshape(D, 3 * D)

    def one_latent(carry, item):
        latent, cond_row, grad_rows = item
        cond_f = cond_row.astype(jnp.float32)
        cond_act = jax.nn.silu(cond_f).astype(jnp.bfloat16)
        modulation = dot32(cond_act[None, :], ada_flat).reshape(6, D) + ada_bias
        latent_f = latent.astype(jnp.float32)
        norm_one, inv_one = norm_rows(latent_f)
        input_one = (norm_one * (1.0 + modulation[1]) + modulation[0]).astype(jnp.bfloat16)
        qkv_all = dot32(input_one, qkv_flat).reshape(SEQ, 3, D)
        queries = (qkv_all[:, 0] + qv_bias[0]).astype(jnp.bfloat16)
        keys_all = qkv_all[:, 1].astype(jnp.bfloat16)
        values_all = (qkv_all[:, 2] + qv_bias[1]).astype(jnp.bfloat16)
        q_heads = as_float(queries).reshape(SEQ, HEADS, HEAD_DIM)
        k_heads = as_float(keys_all).reshape(SEQ, HEADS, HEAD_DIM)
        v_heads = as_float(values_all).reshape(SEQ, HEADS, HEAD_DIM)
        scores = jnp.einsum('qhd,khd->hqk', q_heads, k_heads) * att_scale
        row_max = lax.optimization_barrier(jnp.max(scores, axis=-1, keepdims=True))
        log_total = row_max + jnp.log(lax.optimization_barrier(jnp.sum(jnp.exp(scores - row_max), axis=-1, keepdims=True)))
        soft_probs = jnp.exp(scores - log_total)
        probs_half = as_float(soft_probs.astype(jnp.bfloat16))
        mixed = jnp.einsum('hqk,khd->qhd', probs_half, v_heads).reshape(SEQ, D).astype(jnp.bfloat16)
        attn_val = dot32(mixed, out_weight.T) + out_bias
        after_attn = latent_f + modulation[2] * attn_val
        norm_two, inv_two = norm_rows(after_attn)
        input_two = (norm_two * (1.0 + modulation[4]) + modulation[3]).astype(jnp.bfloat16)
        hidden_pre = dot32(input_two, fc1_weight) + fc1_bias
        hidden_act = gelu_fn(hidden_pre).astype(jnp.bfloat16)
        mlp_val = dot32(hidden_act, fc2_weight.T) + fc2_bias
        block = after_attn + modulation[5] * mlp_val
        grad_gate_two = lax.optimization_barrier(jnp.sum(grad_rows * mlp_val, axis=0))
        grad_mlp = grad_rows * modulation[5]
        bias_fc2 = lax.optimization_barrier(jnp.sum(grad_mlp, axis=0))
        grad_mlp_half = grad_mlp.astype(jnp.bfloat16)
        weight_fc2 = dot32(grad_mlp_half.T, hidden_act)
        grad_act = dot32(grad_mlp_half, fc2_weight)
        grad_pre = jax.vjp(gelu_fn, hidden_pre)[1](grad_act)[0]
        bias_fc1 = lax.optimization_barrier(jnp.sum(grad_pre, axis=0))
        grad_pre_half = grad_pre.astype(jnp.bfloat16)
        weight_fc1 = dot32(input_two.T, grad_pre_half)
        grad_input_two = dot32(grad_pre_half, fc1_weight.T)
        grad_shift_two = lax.optimization_barrier(jnp.sum(grad_input_two, axis=0))
        grad_scale_two = lax.optimization_barrier(jnp.sum(grad_input_two * norm_two, axis=0))
        grad_after = grad_rows + norm_back(grad_input_two * (1.0 + modulation[4]), norm_two, inv_two)
        grad_gate_one = lax.optimization_barrier(jnp.sum(grad_after * attn_val, axis=0))
        grad_attn = grad_after * modulation[2]
        bias_out = lax.optimization_barrier(jnp.sum(grad_attn, axis=0))
        grad_attn_half = grad_attn.astype(jnp.bfloat16)
        weight_out = dot32(grad_attn_half.T, mixed)
        grad_mixed = dot32(grad_attn_half, out_weight).astype(jnp.bfloat16)
        grad_heads = as_float(grad_mixed).reshape(SEQ, HEADS, HEAD_DIM)
        grad_values = jnp.einsum('hqk,qhd->khd', probs_half, grad_heads)
        grad_probs = jnp.einsum('qhd,khd->hqk', grad_heads, v_heads)
        delta = lax.optimization_barrier(jnp.sum(soft_probs * grad_probs, axis=-1, keepdims=True))
        grad_scores = as_float((soft_probs * (grad_probs - delta) * att_scale).astype(jnp.bfloat16))
        grad_queries = jnp.einsum('hqk,khd->qhd', grad_scores, k_heads).reshape(SEQ, D)
        grad_keys = jnp.einsum('hqk,qhd->khd', grad_scores, q_heads).reshape(SEQ, D)
        grad_values = grad_values.reshape(SEQ, D)
        bias_qv = jnp.stack([lax.optimization_barrier(jnp.sum(grad_queries, axis=0)), lax.optimization_barrier(jnp.sum(grad_values, axis=0))])
        grad_qkv = jnp.stack([grad_queries, grad_keys, grad_values], axis=1).astype(jnp.bfloat16).reshape(SEQ, 3 * D)
        weight_qkv = dot32(input_one.T, grad_qkv).reshape(D, 3, D)
        grad_input_one = dot32(grad_qkv, qkv_flat.T)
        grad_shift_one = lax.optimization_barrier(jnp.sum(grad_input_one, axis=0))
        grad_scale_one = lax.optimization_barrier(jnp.sum(grad_input_one * norm_one, axis=0))
        latent_grad = grad_after + norm_back(grad_input_one * (1.0 + modulation[1]), norm_one, inv_one)
        grad_mod = jnp.stack([grad_shift_one, grad_scale_one, grad_gate_one, grad_shift_two, grad_scale_two, grad_gate_two])
        weight_ada = as_float(cond_act)[:, None, None] * grad_mod[None]
        grad_cond_act = jnp.dot(ada_flat.astype(jnp.float32), grad_mod.reshape(6 * D), precision=lax.Precision.HIGHEST)
        cond_grad = jax.vjp(jax.nn.silu, cond_f)[1](grad_cond_act)[0]
        terms = (weight_ada, grad_mod, weight_qkv, bias_qv, weight_out, bias_out, weight_fc1, bias_fc1, weight_fc2, bias_fc2)
        new_carry = tuple((total + term for total, term in zip(carry, terms)))
        return (new_carry, (block, latent_grad, cond_grad))
    start = (jnp.zeros((D, 6, D), jnp.float32), jnp.zeros((6, D), jnp.float32), jnp.zeros((D, 3, D), jnp.float32), jnp.zeros((2, D), jnp.float32), jnp.zeros((D, D), jnp.float32), jnp.zeros((D,), jnp.float32), jnp.zeros((D, FF), jnp.float32), jnp.zeros((FF,), jnp.float32), jnp.zeros((D, FF), jnp.float32), jnp.zeros((D,), jnp.float32))
    totals, outputs = lax.scan(one_latent, start, (latent_in, condition, out_grad))
    blocks, latent_grads, cond_grads = outputs
    return (blocks, latent_grads, cond_grads, totals[0], totals[1], totals[2], totals[3], totals[4], totals[5], totals[6], totals[7], totals[8], totals[9])
```

```python
import jax
import jax.numpy as jnp
from jax import lax
from jax.sharding import PartitionSpec as P

HEAD_DIM = 64


EPS = 1e-06


def dot32(left, right):
    return jnp.dot(left, right, preferred_element_type=jnp.float32)


def rows_inner(left, right):
    return lax.dot_general(
        left, right, (((0,), (0,)), ((), ())), preferred_element_type=jnp.float32
    )


def last_inner(left, right):
    return lax.dot_general(
        left, right, (((left.ndim - 1,), (1,)), ((), ())), preferred_element_type=jnp.float32
    )


def norm_rows(values):
    centre = jnp.mean(values, axis=-1, keepdims=True)
    shifted = values - centre
    spread = jnp.mean(shifted * shifted, axis=-1, keepdims=True)
    inverse = lax.rsqrt(spread + EPS)
    return (shifted * inverse, inverse)


def norm_back(grad_norm, normed, inverse):
    first = jnp.mean(grad_norm, axis=-1, keepdims=True)
    second = jnp.mean(grad_norm * normed, axis=-1, keepdims=True)
    return inverse * (grad_norm - first - normed * second)


def gelu_fn(values):
    return jax.nn.gelu(values, approximate=True)


def shifted(block, axis, step):
    size = lax.axis_size(axis)
    return lax.ppermute(block, axis, [(i, (i + step) % size) for i in range(size)])


def gather(block, axis):
    size = lax.axis_size(axis)
    here = lax.axis_index(axis)
    got = [(here, block)]
    for step in range(1, size):
        got.append((lax.rem(here + size - step, size), shifted(block, axis, step)))
    out = jnp.zeros((size,) + block.shape, block.dtype)
    for place, piece in got:
        out = lax.dynamic_update_index_in_dim(out, piece, place, 0)
    return out


def scatter_sum(terms, axis, wire):
    size = lax.axis_size(axis)
    here = lax.axis_index(axis)
    sent = terms.astype(wire)
    total = lax.dynamic_index_in_dim(terms, here, 0, keepdims=False)
    for step in range(1, size):
        place = lax.rem(here + step, size)
        block = lax.dynamic_index_in_dim(sent, place, 0, keepdims=False)
        total = total + shifted(block, axis, step).astype(jnp.float32)
    return total


def gather_rows(block, axis):
    out = gather(block, axis)
    return out.reshape((-1,) + block.shape[1:])


def to_parts(values, parts):
    lat, seq, width = values.shape
    return values.reshape(lat, parts, seq // parts, width).swapaxes(0, 1)


def from_parts(values):
    parts, lat, seq, width = values.shape
    return values.swapaxes(0, 1).reshape(lat, parts * seq, width)


def own_tokens(values, parts, here):
    return lax.dynamic_slice_in_dim(
        values, here * (values.shape[1] // parts), values.shape[1] // parts, 1
    )


def local(
    latent_in,
    condition,
    ada_weight,
    ada_bias,
    qkv_weight,
    qv_bias,
    out_weight,
    out_bias,
    fc1_weight,
    fc1_bias,
    fc2_weight,
    fc2_bias,
    out_grad,
):
    bf16 = jnp.bfloat16
    f32 = jnp.float32
    tp = lax.axis_size("tp")
    ctx = lax.axis_size("ctx")
    fsdp = lax.axis_size("fsdp")
    tp_here = lax.axis_index("tp")
    fsdp_here = lax.axis_index("fsdp")
    lat_count, seq_part, width_all = latent_in.shape
    rows_here, _, head_cols = qkv_weight.shape
    heads_here = head_cols // HEAD_DIM
    row_count = lat_count * seq_part
    att_scale = HEAD_DIM ** (-0.5)

    cond_f = condition.astype(f32)
    cond_act = jax.nn.silu(cond_f).astype(bf16)
    cond_all = gather_rows(cond_act, "fsdp")
    full_qkv = gather_rows(qkv_weight, "fsdp").reshape(width_all, 3 * head_cols)
    full_out = gather_rows(out_weight, "fsdp")
    full_fc1 = gather_rows(fc1_weight, "fsdp")
    full_fc2 = gather_rows(fc2_weight, "fsdp")

    cond_rows = lax.dynamic_slice_in_dim(cond_all, fsdp_here * rows_here, rows_here, 1)
    mod_terms = dot32(cond_rows, ada_weight.reshape(rows_here, 6 * head_cols))
    mod_cols = scatter_sum(mod_terms.reshape(fsdp, lat_count, 6, head_cols), "fsdp", f32) + ada_bias
    modulation = gather(mod_cols, "tp")
    modulation = modulation.transpose(1, 2, 0, 3).reshape(lat_count, 6, width_all)
    shift_one = modulation[:, 0][:, None, :]
    scale_one = modulation[:, 1][:, None, :]
    gate_one = modulation[:, 2][:, None, :]
    shift_two = modulation[:, 3][:, None, :]
    scale_two = modulation[:, 4][:, None, :]
    gate_two = modulation[:, 5][:, None, :]

    latent_f = latent_in.astype(f32)
    norm_one, inv_one = norm_rows(latent_f)
    input_one = (norm_one * (1.0 + scale_one) + shift_one).astype(bf16)
    qkv_all = dot32(input_one.reshape(row_count, width_all), full_qkv).reshape(
        lat_count, seq_part, 3, head_cols
    )
    queries = (qkv_all[:, :, 0] + qv_bias[0]).astype(bf16)
    keys_local = qkv_all[:, :, 1].astype(bf16)
    values_local = (qkv_all[:, :, 2] + qv_bias[1]).astype(bf16)
    key_value = jnp.stack([keys_local, values_local])
    pieces = [key_value] + [shifted(key_value, "ctx", step) for step in range(1, ctx)]
    key_value = jnp.concatenate(pieces, axis=2)
    seq_whole = ctx * seq_part
    q_heads = queries.reshape(lat_count, seq_part, heads_here, HEAD_DIM)
    k_heads = key_value[0].reshape(lat_count, seq_whole, heads_here, HEAD_DIM)
    v_heads = key_value[1].reshape(lat_count, seq_whole, heads_here, HEAD_DIM)
    scores = (
        jnp.einsum("bqhd,bkhd->bhqk", q_heads, k_heads, preferred_element_type=f32) * att_scale
    )
    row_max = jnp.max(scores, axis=-1, keepdims=True)
    log_total = row_max + jnp.log(jnp.sum(jnp.exp(scores - row_max), axis=-1, keepdims=True))
    probs_half = jnp.exp(scores - log_total).astype(bf16)
    mixed = jnp.einsum("bhqk,bkhd->bqhd", probs_half, v_heads, preferred_element_type=f32)
    mixed = mixed.reshape(lat_count, seq_part, head_cols).astype(bf16)
    attn_term = last_inner(mixed, full_out)

    latent_q = own_tokens(latent_in, tp, tp_here).astype(f32)
    norm_one_q, inv_one_q = norm_rows(latent_q)
    out_grad_q = own_tokens(out_grad, tp, tp_here)
    attn_val = scatter_sum(to_parts(attn_term, tp), "tp", bf16) + out_bias
    after_attn = latent_q + gate_one * attn_val
    norm_two, inv_two = norm_rows(after_attn)
    input_two = (norm_two * (1.0 + scale_two) + shift_two).astype(bf16)
    input_two = from_parts(gather(input_two, "tp")).reshape(row_count, width_all)
    hidden_pre = dot32(input_two, full_fc1) + fc1_bias
    hidden_act = gelu_fn(hidden_pre).astype(bf16)

    grad_mlp_half = (out_grad * gate_two).astype(bf16).reshape(row_count, width_all)
    grad_act = dot32(grad_mlp_half, full_fc2)
    grad_pre = jax.vjp(gelu_fn, hidden_pre)[1](grad_act)[0]
    bias_fc1 = jnp.sum(grad_pre, axis=0)
    grad_pre_half = grad_pre.astype(bf16)
    input_two_term = last_inner(grad_pre_half, full_fc1).reshape(lat_count, seq_part, width_all)
    grad_input_two = scatter_sum(to_parts(input_two_term, tp), "tp", bf16)

    mlp_term = last_inner(hidden_act, full_fc2).reshape(lat_count, seq_part, width_all)
    mlp_val = scatter_sum(to_parts(mlp_term, tp), "tp", bf16) + fc2_bias
    block_out = after_attn + gate_two * mlp_val
    block_out = from_parts(gather(block_out.astype(bf16), "tp")).astype(f32)
    fc2_term = rows_inner(grad_mlp_half, hidden_act)
    fc1_term = rows_inner(input_two, grad_pre_half)

    def reduce_weight(term):
        flat = term.reshape(fsdp, rows_here, -1)
        part = scatter_sum(flat, "fsdp", bf16)
        part = scatter_sum(part.reshape(ctx, rows_here // ctx, -1), "ctx", bf16)
        return gather_rows(part.astype(bf16), "ctx").astype(f32)

    grad_gate_two = jnp.sum(out_grad_q * mlp_val, axis=1)
    bias_fc2 = jnp.sum(out_grad_q * gate_two, axis=(0, 1))
    grad_shift_two = jnp.sum(grad_input_two, axis=1)
    grad_scale_two = jnp.sum(grad_input_two * norm_two, axis=1)
    grad_after = out_grad_q + norm_back(grad_input_two * (1.0 + scale_two), norm_two, inv_two)
    grad_gate_one = jnp.sum(grad_after * attn_val, axis=1)
    grad_attn = grad_after * gate_one
    bias_out = jnp.sum(grad_attn, axis=(0, 1))
    grad_attn_half = from_parts(gather(grad_attn.astype(bf16), "tp")).reshape(row_count, width_all)
    out_term = rows_inner(grad_attn_half, mixed.reshape(row_count, head_cols))
    grad_mixed = (
        dot32(grad_attn_half, full_out)
        .astype(bf16)
        .reshape(lat_count, seq_part, heads_here, HEAD_DIM)
    )
    soft_probs = jnp.exp(scores - log_total)
    grad_v_whole = jnp.einsum("bhqk,bqhd->bkhd", probs_half, grad_mixed, preferred_element_type=f32)
    grad_probs = jnp.einsum("bqhd,bkhd->bhqk", grad_mixed, v_heads, preferred_element_type=f32)
    delta = jnp.sum(soft_probs * grad_probs, axis=-1, keepdims=True)
    grad_scores = (soft_probs * (grad_probs - delta) * att_scale).astype(bf16)
    grad_queries = jnp.einsum(
        "bhqk,bkhd->bqhd", grad_scores, k_heads, preferred_element_type=f32
    ).reshape(lat_count, seq_part, head_cols)
    grad_k_whole = jnp.einsum("bhqk,bqhd->bkhd", grad_scores, q_heads, preferred_element_type=f32)
    grad_k_whole = grad_k_whole.reshape(lat_count, seq_whole, head_cols)
    grad_v_whole = grad_v_whole.reshape(lat_count, seq_whole, head_cols)
    bias_qv = jnp.stack([jnp.sum(grad_queries, axis=(0, 1)), jnp.sum(grad_v_whole, axis=(0, 1))])

    def home(whole):
        total = whole[:, :seq_part]
        for step in range(1, ctx):
            block = whole[:, step * seq_part : (step + 1) * seq_part].astype(bf16)
            total = total + shifted(block, "ctx", ctx - step).astype(f32)
        return total

    grad_qkv = (
        jnp.stack([grad_queries, home(grad_k_whole), home(grad_v_whole)], axis=2)
        .astype(bf16)
        .reshape(row_count, 3 * head_cols)
    )
    qkv_term = rows_inner(input_one.reshape(row_count, width_all), grad_qkv)
    input_one_term = last_inner(grad_qkv, full_qkv).reshape(lat_count, seq_part, width_all)
    grad_input_one = scatter_sum(to_parts(input_one_term, tp), "tp", bf16)
    grad_shift_one = jnp.sum(grad_input_one, axis=1)
    grad_scale_one = jnp.sum(grad_input_one * norm_one_q, axis=1)
    latent_grad = grad_after + norm_back(
        grad_input_one * (1.0 + scale_one), norm_one_q, inv_one_q
    )
    latent_grad = from_parts(gather(latent_grad.astype(bf16), "tp")).astype(f32)

    small = jnp.concatenate(
        [
            jnp.stack(
                [
                    grad_shift_one,
                    grad_scale_one,
                    grad_gate_one,
                    grad_shift_two,
                    grad_scale_two,
                    grad_gate_two,
                ],
                axis=1,
            ).reshape(lat_count * 6, width_all),
            bias_out[None],
            bias_fc2[None],
        ]
    )
    small = scatter_sum(small.reshape(-1, tp, head_cols).swapaxes(0, 1), "tp", f32)
    small = jnp.concatenate([small, bias_qv, bias_fc1.reshape(-1, head_cols)])
    small = gather(jnp.sum(gather(small, "ctx"), axis=0), "fsdp")
    grad_mod = small[:, : lat_count * 6].reshape(fsdp * lat_count, 6, head_cols)
    bias_sums = jnp.sum(small[:, lat_count * 6 :], axis=0)
    bias_ada = jnp.sum(grad_mod, axis=0)
    bias_qv = bias_sums[2:4]
    bias_fc1 = bias_sums[4:].reshape(-1)
    cond_term = jnp.einsum(
        "bje,dje->bd", grad_mod, ada_weight.astype(f32), precision=lax.Precision.HIGHEST
    )
    last = jnp.concatenate([cond_term.reshape(-1), bias_sums[:2].reshape(-1)])
    last = gather(last, "tp")
    bias_both = last[:, cond_term.size :].reshape(tp, 2, head_cols).swapaxes(0, 1)
    bias_both = bias_both.reshape(2, width_all)
    cond_term = jnp.sum(last[:, : cond_term.size], axis=0).reshape(cond_term.shape)
    cond_term = gather(cond_term, "fsdp")
    cond_term = lax.dynamic_slice_in_dim(cond_term, fsdp_here * lat_count, lat_count, 1)
    grad_cond_act = cond_term.swapaxes(0, 1).reshape(lat_count, width_all)
    condition_grad = jax.vjp(jax.nn.silu, cond_f)[1](grad_cond_act)[0]
    ada_grad = jnp.einsum(
        "bd,bje->dje", cond_rows.astype(f32), grad_mod, precision=lax.Precision.HIGHEST
    )
    return (
        block_out,
        latent_grad,
        condition_grad,
        ada_grad,
        bias_ada,
        reduce_weight(qkv_term).reshape(rows_here, 3, head_cols),
        bias_qv,
        reduce_weight(out_term),
        bias_both[0],
        reduce_weight(fc1_term),
        bias_fc1,
        reduce_weight(fc2_term),
        bias_both[1],
    )


def solution(mesh):
    placed = (
        P("fsdp", "ctx", None),
        P("fsdp", None),
        P("fsdp", None, "tp"),
        P(None, "tp"),
        P("fsdp", None, "tp"),
        P(None, "tp"),
        P("fsdp", "tp"),
        P(),
        P("fsdp", "tp"),
        P("tp"),
        P("fsdp", "tp"),
        P(),
        P("fsdp", "ctx", None),
    )
    return jax.shard_map(
        local,
        mesh=mesh,
        in_specs=placed,
        out_specs=(
            P("fsdp", "ctx", None),
            P("fsdp", "ctx", None),
            P("fsdp", None),
            P("fsdp", None, "tp"),
            P(None, "tp"),
            P("fsdp", None, "tp"),
            P(None, "tp"),
            P("fsdp", "tp"),
            P(),
            P("fsdp", "tp"),
            P("tp"),
            P("fsdp", "tp"),
            P(),
        ),
        check_vma=False,
    )
```

```python
import functools
import itertools

import jax
import jax.numpy as jnp
from jax import lax
from jax.experimental import pallas as pl
from jax.experimental.pallas import tpu as pltpu
from jax.sharding import PartitionSpec as P

HEAD_DIM = 64


EPS = 1e-06


def dot32(left, right):
    return jnp.dot(left, right, preferred_element_type=jnp.float32)


def rows_inner(left, right):
    return lax.dot_general(
        left, right, (((0,), (0,)), ((), ())), preferred_element_type=jnp.float32
    )


def last_inner(left, right):
    return lax.dot_general(
        left, right, (((left.ndim - 1,), (1,)), ((), ())), preferred_element_type=jnp.float32
    )


def norm_rows(values):
    centre = jnp.mean(values, axis=-1, keepdims=True)
    shifted = values - centre
    spread = jnp.mean(shifted * shifted, axis=-1, keepdims=True)
    inverse = lax.rsqrt(spread + EPS)
    return (shifted * inverse, inverse)


def norm_back(grad_norm, normed, inverse):
    first = jnp.mean(grad_norm, axis=-1, keepdims=True)
    second = jnp.mean(grad_norm * normed, axis=-1, keepdims=True)
    return inverse * (grad_norm - first - normed * second)


def gelu_fn(values):
    return jax.nn.gelu(values, approximate=True)


def shifted(block, axis, step):
    size = lax.axis_size(axis)
    return lax.ppermute(block, axis, [(i, (i + step) % size) for i in range(size)])


def gather_rows(block, axis):
    size = lax.axis_size(axis)
    here = lax.axis_index(axis)
    rows = block.shape[0]
    cycle = [shifted(block, axis, step) for step in range(size - 1, 0, -1)] + [block]
    twice = jnp.concatenate(cycle + cycle[:-1])
    return lax.dynamic_slice_in_dim(twice, (size - 1 - here) * rows, size * rows, 0)


def scatter_rows(terms, axis):
    size = lax.axis_size(axis)
    here = lax.axis_index(axis)
    sent = terms.astype(jnp.bfloat16)
    total = lax.dynamic_index_in_dim(terms, here, 0, keepdims=False).astype(jnp.float32)
    for step in range(1, size):
        place = lax.rem(here + step, size)
        block = lax.dynamic_index_in_dim(sent, place, 0, keepdims=False)
        total = total + shifted(block, axis, step).astype(jnp.float32)
    return total


def part_of(ref, dim, place, length):
    start = place * length
    if dim == 0:
        return ref.at[pl.ds(start, length)]
    return ref.at[:, pl.ds(pl.multiple_of(start, length), length)]


def greet(axis, size, here):
    barrier = pltpu.get_barrier_semaphore()
    for step in range(1, size):
        pl.semaphore_signal(
            barrier,
            inc=1,
            device_id={axis: lax.rem(here + step, size)},
            device_id_type=pl.DeviceIdType.MESH,
        )
    pl.semaphore_wait(barrier, size - 1)


def gather_kernel(axis, size, dim, block_ref, out_ref, send_sem, recv_sem, own_sem):
    here = lax.axis_index(axis)
    length = block_ref.shape[dim]
    greet(axis, size, here)
    copies = [
        pltpu.make_async_remote_copy(
            src_ref=block_ref,
            dst_ref=part_of(out_ref, dim, here, length),
            send_sem=send_sem.at[step - 1],
            recv_sem=recv_sem.at[step - 1],
            device_id={axis: lax.rem(here + step, size)},
            device_id_type=pl.DeviceIdType.MESH,
        )
        for step in range(1, size)
    ]
    for copy in copies:
        copy.start()
    own = pltpu.make_async_copy(block_ref, part_of(out_ref, dim, here, length), own_sem)
    own.start()
    own.wait()
    for copy in copies:
        copy.wait()


def scatter_kernel(axis, size, dim, terms_ref, out_ref, send_sem, recv_sem):
    here = lax.axis_index(axis)
    length = terms_ref.shape[dim] // size
    greet(axis, size, here)
    copies = []
    for step in range(1, size):
        peer = lax.rem(here + step, size)
        copies.append(
            pltpu.make_async_remote_copy(
                src_ref=part_of(terms_ref, dim, peer, length),
                dst_ref=out_ref.at[step - 1],
                send_sem=send_sem.at[step - 1],
                recv_sem=recv_sem.at[step - 1],
                device_id={axis: peer},
                device_id_type=pl.DeviceIdType.MESH,
            )
        )
        copies[-1].start()
    for copy in copies:
        copy.wait()


def exchange(kernel, operand, shape, size, ids, own):
    sems = [pltpu.SemaphoreType.DMA((size - 1,))] * 2
    return pl.pallas_call(
        kernel,
        out_shape=jax.ShapeDtypeStruct(shape, operand.dtype),
        in_specs=[pl.BlockSpec(memory_space=pltpu.VMEM)],
        out_specs=pl.BlockSpec(memory_space=pltpu.VMEM),
        scratch_shapes=sems + ([pltpu.SemaphoreType.DMA] if own else []),
        compiler_params=pltpu.CompilerParams(collective_id=next(ids), has_side_effects=True),
        cost_estimate=pl.CostEstimate(flops=0, bytes_accessed=20_000_000, transcendentals=0),
    )(operand)


def gather(block, axis, dim, ids):
    size = lax.axis_size(axis)
    shape = list(block.shape)
    shape[dim] *= size
    kernel = functools.partial(gather_kernel, axis, size, dim)
    return exchange(kernel, block, tuple(shape), size, ids, True)


def scatter_sum(terms, axis, dim, ids, wire):
    size = lax.axis_size(axis)
    shape = list(terms.shape)
    shape[dim] //= size
    kernel = functools.partial(scatter_kernel, axis, size, dim)
    got = exchange(kernel, terms.astype(wire), (size - 1, *shape), size, ids, False)
    own = lax.dynamic_slice_in_dim(terms, lax.axis_index(axis) * shape[dim], shape[dim], dim)
    return own + jnp.sum(got.astype(jnp.float32), axis=0)


def own_tokens(values, parts, here):
    return lax.dynamic_slice_in_dim(
        values, here * (values.shape[1] // parts), values.shape[1] // parts, 1
    )


def local(
    latent_in,
    condition,
    ada_weight,
    ada_bias,
    qkv_weight,
    qv_bias,
    out_weight,
    out_bias,
    fc1_weight,
    fc1_bias,
    fc2_weight,
    fc2_bias,
    out_grad,
):
    bf16 = jnp.bfloat16
    ids = itertools.count()
    f32 = jnp.float32
    tp = lax.axis_size("tp")
    ctx = lax.axis_size("ctx")
    fsdp = lax.axis_size("fsdp")
    tp_here = lax.axis_index("tp")
    fsdp_here = lax.axis_index("fsdp")
    lat_count, seq_part, width_all = latent_in.shape
    rows_here, _, head_cols = qkv_weight.shape
    heads_here = head_cols // HEAD_DIM
    row_count = lat_count * seq_part
    att_scale = HEAD_DIM ** (-0.5)

    cond_f = condition.astype(f32)
    cond_act = jax.nn.silu(cond_f).astype(bf16)
    full_qkv = gather_rows(qkv_weight.reshape(rows_here, 3 * head_cols), "fsdp")
    full_qkv, rest = lax.optimization_barrier((full_qkv, (out_weight, fc1_weight, fc2_weight)))
    full_out = gather_rows(rest[0], "fsdp")
    full_fc1 = gather_rows(rest[1], "fsdp")
    full_fc2 = gather_rows(rest[2], "fsdp")
    cond_all = gather(cond_act.astype(f32)[None], "fsdp", 0, ids)
    cond_all = cond_all.reshape(fsdp * lat_count, width_all).astype(bf16)

    cond_rows = lax.dynamic_slice_in_dim(cond_all, fsdp_here * rows_here, rows_here, 1)
    mod_terms = dot32(cond_rows, ada_weight.reshape(rows_here, 6 * head_cols))
    mod_cols = scatter_sum(
        mod_terms.reshape(fsdp, lat_count * 6, head_cols), "fsdp", 0, ids, f32
    ).reshape(lat_count, 6, head_cols)
    mod_cols = mod_cols + ada_bias
    modulation = gather(mod_cols.reshape(1, lat_count * 6, head_cols), "tp", 0, ids)
    modulation = modulation.reshape(tp, lat_count, 6, head_cols)
    modulation = modulation.transpose(1, 2, 0, 3).reshape(lat_count, 6, width_all)
    shift_one = modulation[:, 0][:, None, :]
    scale_one = modulation[:, 1][:, None, :]
    gate_one = modulation[:, 2][:, None, :]
    shift_two = modulation[:, 3][:, None, :]
    scale_two = modulation[:, 4][:, None, :]
    gate_two = modulation[:, 5][:, None, :]

    latent_f = latent_in.astype(f32)
    norm_one, inv_one = norm_rows(latent_f)
    input_one = (norm_one * (1.0 + scale_one) + shift_one).astype(bf16)
    qkv_all = dot32(input_one.reshape(row_count, width_all), full_qkv).reshape(
        lat_count, seq_part, 3, head_cols
    )
    queries = (qkv_all[:, :, 0] + qv_bias[0]).astype(bf16)
    keys_local = qkv_all[:, :, 1].astype(bf16)
    values_local = (qkv_all[:, :, 2] + qv_bias[1]).astype(bf16)
    key_value = jnp.stack([keys_local, values_local])
    pieces = [key_value] + [shifted(key_value, "ctx", step) for step in range(1, ctx)]
    key_value = jnp.concatenate(pieces, axis=2)
    seq_whole = ctx * seq_part
    q_heads = queries.reshape(lat_count, seq_part, heads_here, HEAD_DIM)
    k_heads = key_value[0].reshape(lat_count, seq_whole, heads_here, HEAD_DIM)
    v_heads = key_value[1].reshape(lat_count, seq_whole, heads_here, HEAD_DIM)
    scores = (
        jnp.einsum("bqhd,bkhd->bhqk", q_heads, k_heads, preferred_element_type=f32) * att_scale
    )
    row_max = jnp.max(scores, axis=-1, keepdims=True)
    log_total = row_max + jnp.log(jnp.sum(jnp.exp(scores - row_max), axis=-1, keepdims=True))
    probs_half = jnp.exp(scores - log_total).astype(bf16)
    mixed = jnp.einsum("bhqk,bkhd->bqhd", probs_half, v_heads, preferred_element_type=f32)
    mixed = mixed.reshape(lat_count, seq_part, head_cols).astype(bf16)
    attn_term = last_inner(mixed, full_out)

    latent_q = own_tokens(latent_in, tp, tp_here).astype(f32)
    norm_one_q, inv_one_q = norm_rows(latent_q)
    out_grad_q = own_tokens(out_grad, tp, tp_here)
    attn_val = scatter_sum(attn_term, "tp", 1, ids, bf16) + out_bias
    after_attn = latent_q + gate_one * attn_val
    norm_two, inv_two = norm_rows(after_attn)
    input_two = (norm_two * (1.0 + scale_two) + shift_two).astype(bf16)
    input_two = gather(input_two, "tp", 1, ids).reshape(row_count, width_all)
    hidden_pre = dot32(input_two, full_fc1) + fc1_bias
    hidden_act = gelu_fn(hidden_pre).astype(bf16)

    grad_mlp_half = (out_grad * gate_two).astype(bf16).reshape(row_count, width_all)
    grad_act = dot32(grad_mlp_half, full_fc2)
    grad_pre = jax.vjp(gelu_fn, hidden_pre)[1](grad_act)[0]
    bias_fc1 = jnp.sum(grad_pre, axis=0)
    grad_pre_half = grad_pre.astype(bf16)
    input_two_term = last_inner(grad_pre_half, full_fc1).reshape(lat_count, seq_part, width_all)
    grad_input_two = scatter_sum(input_two_term, "tp", 1, ids, bf16)

    mlp_term = last_inner(hidden_act, full_fc2).reshape(lat_count, seq_part, width_all)
    mlp_val = scatter_sum(mlp_term, "tp", 1, ids, bf16) + fc2_bias
    block_out = after_attn + gate_two * mlp_val
    block_out = gather(block_out.astype(bf16), "tp", 1, ids).astype(f32)
    fc2_term = rows_inner(grad_mlp_half, hidden_act)
    fc1_term = rows_inner(input_two, grad_pre_half)

    def reduce_weights(*terms):
        flat = jnp.concatenate([term.astype(bf16) for term in terms], axis=1)
        part = scatter_rows(flat.reshape(fsdp, rows_here, -1), "fsdp")
        part = scatter_rows(part.reshape(ctx, rows_here // ctx, -1), "ctx")
        return gather_rows(part.astype(bf16), "ctx")

    fc_grads = reduce_weights(fc1_term, fc2_term)
    ff_cols = fc1_term.shape[1]

    grad_gate_two = jnp.sum(out_grad_q * mlp_val, axis=1)
    bias_fc2 = jnp.sum(out_grad_q * gate_two, axis=(0, 1))
    grad_shift_two = jnp.sum(grad_input_two, axis=1)
    grad_scale_two = jnp.sum(grad_input_two * norm_two, axis=1)
    grad_after = out_grad_q + norm_back(grad_input_two * (1.0 + scale_two), norm_two, inv_two)
    grad_gate_one = jnp.sum(grad_after * attn_val, axis=1)
    grad_attn = grad_after * gate_one
    bias_out = jnp.sum(grad_attn, axis=(0, 1))
    grad_attn_half = gather(grad_attn.astype(bf16), "tp", 1, ids).reshape(row_count, width_all)
    out_term = rows_inner(grad_attn_half, mixed.reshape(row_count, head_cols))
    grad_mixed = (
        dot32(grad_attn_half, full_out)
        .astype(bf16)
        .reshape(lat_count, seq_part, heads_here, HEAD_DIM)
    )
    soft_probs = jnp.exp(scores - log_total)
    grad_v_whole = jnp.einsum("bhqk,bqhd->bkhd", probs_half, grad_mixed, preferred_element_type=f32)
    grad_probs = jnp.einsum("bqhd,bkhd->bhqk", grad_mixed, v_heads, preferred_element_type=f32)
    delta = jnp.sum(soft_probs * grad_probs, axis=-1, keepdims=True)
    grad_scores = (soft_probs * (grad_probs - delta) * att_scale).astype(bf16)
    grad_queries = jnp.einsum(
        "bhqk,bkhd->bqhd", grad_scores, k_heads, preferred_element_type=f32
    ).reshape(lat_count, seq_part, head_cols)
    grad_k_whole = jnp.einsum("bhqk,bqhd->bkhd", grad_scores, q_heads, preferred_element_type=f32)
    grad_k_whole = grad_k_whole.reshape(lat_count, seq_whole, head_cols)
    grad_v_whole = grad_v_whole.reshape(lat_count, seq_whole, head_cols)
    bias_qv = jnp.stack([jnp.sum(grad_queries, axis=(0, 1)), jnp.sum(grad_v_whole, axis=(0, 1))])

    def home(whole):
        total = whole[:, :seq_part]
        for step in range(1, ctx):
            block = whole[:, step * seq_part : (step + 1) * seq_part].astype(bf16)
            total = total + shifted(block, "ctx", ctx - step).astype(f32)
        return total

    grad_qkv = (
        jnp.stack([grad_queries, home(grad_k_whole), home(grad_v_whole)], axis=2)
        .astype(bf16)
        .reshape(row_count, 3 * head_cols)
    )
    qkv_term = rows_inner(input_one.reshape(row_count, width_all), grad_qkv)
    late_grads = reduce_weights(out_term, qkv_term)
    input_one_term = last_inner(grad_qkv, full_qkv).reshape(lat_count, seq_part, width_all)
    grad_input_one = scatter_sum(input_one_term, "tp", 1, ids, bf16)
    grad_shift_one = jnp.sum(grad_input_one, axis=1)
    grad_scale_one = jnp.sum(grad_input_one * norm_one_q, axis=1)
    latent_grad = grad_after + norm_back(
        grad_input_one * (1.0 + scale_one), norm_one_q, inv_one_q
    )
    latent_grad = gather(latent_grad.astype(bf16), "tp", 1, ids).astype(f32)

    small = jnp.concatenate(
        [
            jnp.stack(
                [
                    grad_shift_one,
                    grad_scale_one,
                    grad_gate_one,
                    grad_shift_two,
                    grad_scale_two,
                    grad_gate_two,
                ],
                axis=1,
            ).reshape(lat_count * 6, width_all),
            bias_out[None],
            bias_fc2[None],
        ]
    )
    small = scatter_sum(small.reshape(-1, tp, head_cols).swapaxes(0, 1), "tp", 0, ids, f32)[0]
    small = jnp.concatenate([small, bias_qv, bias_fc1.reshape(-1, head_cols)])
    small = jnp.sum(gather(small[None], "ctx", 0, ids), axis=0)
    small = gather(small[None], "fsdp", 0, ids)
    grad_mod = small[:, : lat_count * 6].reshape(fsdp * lat_count, 6, head_cols)
    bias_sums = jnp.sum(small[:, lat_count * 6 :], axis=0)
    bias_ada = jnp.sum(grad_mod, axis=0)
    bias_qv = bias_sums[2:4]
    bias_fc1 = bias_sums[4:].reshape(-1)
    cond_term = jnp.einsum(
        "bje,dje->bd", grad_mod, ada_weight.astype(f32), precision=lax.Precision.HIGHEST
    )
    last = jnp.concatenate([cond_term.reshape(-1), bias_sums[:2].reshape(-1)])
    last = gather(last[None, None], "tp", 0, ids)[:, 0]
    bias_both = last[:, cond_term.size :].reshape(tp, 2, head_cols).swapaxes(0, 1)
    bias_both = bias_both.reshape(2, width_all)
    cond_term = jnp.sum(last[:, : cond_term.size], axis=0).reshape(cond_term.shape)
    cond_term = gather(cond_term[None], "fsdp", 0, ids)
    cond_term = lax.dynamic_slice_in_dim(cond_term, fsdp_here * lat_count, lat_count, 1)
    grad_cond_act = cond_term.swapaxes(0, 1).reshape(lat_count, width_all)
    condition_grad = jax.vjp(jax.nn.silu, cond_f)[1](grad_cond_act)[0]
    ada_grad = jnp.einsum(
        "bd,bje->dje", cond_rows.astype(f32), grad_mod, precision=lax.Precision.HIGHEST
    )
    return (
        block_out,
        latent_grad,
        condition_grad,
        ada_grad,
        bias_ada,
        late_grads[:, head_cols:].astype(f32).reshape(rows_here, 3, head_cols),
        bias_qv,
        late_grads[:, :head_cols].astype(f32),
        bias_both[0],
        fc_grads[:, :ff_cols].astype(f32),
        bias_fc1,
        fc_grads[:, ff_cols:].astype(f32),
        bias_both[1],
    )


def solution(mesh):
    placed = (
        P("fsdp", "ctx", None),
        P("fsdp", None),
        P("fsdp", None, "tp"),
        P(None, "tp"),
        P("fsdp", None, "tp"),
        P(None, "tp"),
        P("fsdp", "tp"),
        P(),
        P("fsdp", "tp"),
        P("tp"),
        P("fsdp", "tp"),
        P(),
        P("fsdp", "ctx", None),
    )
    return jax.shard_map(
        local,
        mesh=mesh,
        in_specs=placed,
        out_specs=(
            P("fsdp", "ctx", None),
            P("fsdp", "ctx", None),
            P("fsdp", None),
            P("fsdp", None, "tp"),
            P(None, "tp"),
            P("fsdp", None, "tp"),
            P(None, "tp"),
            P("fsdp", "tp"),
            P(),
            P("fsdp", "tp"),
            P("tp"),
            P("fsdp", "tp"),
            P(),
        ),
        check_vma=False,
    )
```
